32 devices in a mesh: gx: 4 (over y, x), gy: 8 (over z, core).
Axes of the slice: x: 2, y: 2, z: 4, core: 2. Of those that a mesh axis runs over, the one named last changes fastest.
Arguments:
- start_block: bfloat16 [64, 65536], P(None, ('gx', 'gy')), may hold values from -200 to 200
- tiles: bfloat16 [256, 10, 256, 256], P(('gx', 'gy')), may hold values from -0.125 to 0.125
- tile_cols: int32 [256, 10], P(('gx', 'gy')), may hold values from 0 to 15, as said below
- send_rows: int32 [32, 2], P(('gx', 'gy')), may hold values from 0 to 7, as said below
- shifts: float32 [4], replicated, may hold values from -1 to 1
Outputs:
- basis_q: float32 [256, 65536], P(None, ('gx', 'gy'))
The draws below stay inside these ranges and needn't reach their ends.
Inputs may be any that keep to these rules, and one draw needn't show every extreme that they name: `tile_cols`: every tile-row's first tile is its own diagonal tile; values below 8 name the partition's own tile-rows, the others ghost slots in the extended order. `send_rows`: each partition's 2 entries are distinct own tile-rows.
All inputs are finite; a program needn't handle non-finite values.
Results may differ from the reference program's by a relative error of at most 0.009.
The reference program's roundings to bfloat16 on the way count: a program that leaves them out, or rounds other values in their place, can miss the bound.
Values may be sent and summed in bfloat16 or wider, within the bound.
A program may use at most 64 MiB of HBM per device.

```python
import jax
import jax.numpy as jnp
from jax import lax

TILE = 256
BLOCK = 64
STEPS = 4
TR_DEV = 8
K = 10
GHOSTS = 2
NT = 256
NROWS = 65536
N_GX = 4
N_GY = 8
DEVICES = 32


def draw_start_block(key, part):
    noise_key = jax.random.fold_in(key, 0)
    values = jnp.clip(jax.random.normal(noise_key, (BLOCK, NROWS), jnp.float32), -6.0, 6.0)
    return values.astype(jnp.bfloat16)


def draw_tile_cols(key, part):
    local = jnp.arange(NT, dtype=jnp.int32) % TR_DEV
    first = local[:, None]
    second = (TR_DEV + local % (4 * GHOSTS))[:, None]
    rest = jax.random.randint(key, (NT, K - 2), 0, TR_DEV + 4 * GHOSTS, dtype=jnp.int32)
    return jnp.concatenate([first, second, rest], axis=1).astype(jnp.int32)


def draw_send_rows(key, part):
    keys = jax.random.split(key, DEVICES)
    perms = jax.vmap(lambda k: jax.random.permutation(k, TR_DEV))(keys).astype(jnp.int32)
    chosen = perms[:, :GHOSTS]
    fixed_row = jnp.roll(jnp.arange(TR_DEV, dtype=jnp.int32), 1)[:GHOSTS]
    return chosen.at[0].set(fixed_row).astype(jnp.int32)


def level_of(stream_key, extent, cuts, least, top_value):
    factor_of, own = 1.0, jax.random.fold_in(stream_key, 6)
    for axis_at, blocks in cuts:
        heights = jnp.exp(jax.random.uniform(jax.random.fold_in(own, axis_at), (blocks,), jnp.float32, least / len(cuts), top_value / len(cuts)))
        factor_of = factor_of * jnp.repeat(heights, extent[axis_at] // blocks).reshape([-1 if axis == axis_at else 1 for axis in range(len(extent))])
    return factor_of


def scatter_about(rng, extent, deviation, limit, pieces=(), kind=jnp.bfloat16):
    array = deviation * jax.random.normal(rng, extent, jnp.float32)
    if pieces:
        array = array * level_of(rng, extent, pieces, -0.22, 0.18)
    return jnp.clip(array, -limit, limit).astype(kind)


def setup_inputs(seed: int = 0) -> dict:
    key_list = jax.random.split(jax.random.key(seed), 6)
    start_block = draw_start_block(jax.random.fold_in(key_list[5], 71), 0)
    tiles = scatter_about(key_list[1], (NT, K, TILE, TILE), (TILE * K) ** -0.5, 0.125, ((0, 32),))
    tile_cols = draw_tile_cols(jax.random.fold_in(key_list[5], 71), 0)
    send_rows = draw_send_rows(jax.random.fold_in(key_list[5], 71), 0)
    shifts = jnp.clip(jax.random.uniform(key_list[4], (STEPS,), jnp.float32, -1.0, 1.0), -1.0, 1.0)
    return dict(start_block=start_block, tiles=tiles, tile_cols=tile_cols, send_rows=send_rows, shifts=shifts)


def apply_operator(current, tiles, tile_cols, send_rows):
    parts = N_GX * N_GY
    own = current.reshape(BLOCK, parts, TR_DEV, TILE)
    flat = (jnp.arange(parts, dtype=jnp.int32)[:, None] * TR_DEV + send_rows).reshape(-1).astype(jnp.int32)
    outgoing = jnp.take(own.reshape(BLOCK, parts * TR_DEV, TILE), flat, axis=1)
    outgoing = outgoing.reshape(BLOCK, N_GX, N_GY, GHOSTS, TILE)
    padded = jnp.pad(outgoing, ((0, 0), (1, 1), (1, 1), (0, 0), (0, 0)))
    from_xm = padded[:, :-2, 1:-1]
    from_xp = padded[:, 2:, 1:-1]
    from_ym = padded[:, 1:-1, :-2]
    from_yp = padded[:, 1:-1, 2:]
    own_grid = own.reshape(BLOCK, N_GX, N_GY, TR_DEV, TILE)
    extended = jnp.concatenate([own_grid, from_xm, from_xp, from_ym, from_yp], axis=3)
    extended = extended.reshape(BLOCK, parts, TR_DEV + 4 * GHOSTS, TILE)
    cols = tile_cols.reshape(parts, TR_DEV * K)
    tile_parts = tiles.reshape(parts, TR_DEV, K, TILE, TILE)

    def apply_part(index):
        ext = lax.dynamic_index_in_dim(extended, index, 1, keepdims=False)
        picked = jnp.take(ext, cols[index], axis=1).reshape(BLOCK, TR_DEV, K, TILE)
        return jnp.einsum('ctkb,tkab->cta', picked.astype(jnp.float32), tile_parts[index].astype(jnp.float32), precision=lax.Precision.HIGHEST)
    image = lax.map(apply_part, jnp.arange(parts, dtype=jnp.int32))
    return jnp.transpose(image, (1, 0, 2, 3)).reshape(BLOCK, NROWS)

def reference(start_block, tiles, tile_cols, send_rows, shifts):
    current = start_block
    blocks = []
    for step in range(STEPS):
        image = apply_operator(current, tiles, tile_cols, send_rows)
        current = (image - shifts[step] * current.astype(jnp.float32)).astype(jnp.bfloat16)
        blocks.append(current)
    basis = jnp.concatenate(blocks, axis=0)
    gram = lax.dot_general(basis.astype(jnp.float32), basis.astype(jnp.float32), (((1,), (1,)), ((), ())), preferred_element_type=jnp.float32) / NROWS
    lower = jnp.linalg.cholesky(gram)
    return lax.linalg.triangular_solve(lower, basis.astype(jnp.float32), left_side=True, lower=True)
```

```python
import functools

import jax
import jax.numpy as jnp
from jax import lax
from jax.experimental import pallas as pl
from jax.experimental.pallas import tpu as pltpu
from jax.sharding import PartitionSpec as P

MESH = pl.DeviceIdType.MESH
F32 = jnp.float32
BF16 = jnp.bfloat16
NT_DIMS = (((1,), (1,)), ((), ()))


def nt(a, b, precision=None):
    return lax.dot_general(a, b, NT_DIMS, precision=precision, preferred_element_type=F32)


def krylov_kernel(dims, send_rows, tile_cols, shifts, start, tiles_hbm, basis, gram, *scratch):
    nx, ny, steps, tile_rows, slots, ghosts, tile, width, total = dims
    tiles, tile_sem = scratch[0:2]
    halo_send, halo_recv, rs_send, rs_recv, xs_send, xs_recv, ag_send, ag_recv = scratch[2:10]
    at = 10
    ext = scratch[at:at + steps]
    outbox = scratch[at + steps:at + 2 * steps]
    part = scratch[at + 2 * steps:at + 3 * steps]
    rs = scratch[at + 3 * steps:at + 4 * steps]
    xs = scratch[at + 4 * steps:at + 5 * steps]
    full = scratch[at + 5 * steps:at + 6 * steps]
    first = scratch[at + 6 * steps]
    piece = width // ny
    ix, iy = lax.axis_index("gx"), lax.axis_index("gy")

    def tile_copy(t):
        return pltpu.make_async_copy(tiles_hbm.at[t], tiles.at[t], tile_sem.at[t])

    for t in range(tile_rows):
        tile_copy(t).start()

    for s in range(steps):
        ext[s][tile_rows:] = jnp.zeros(ext[s][tile_rows:].shape, BF16)

    barrier = pltpu.get_barrier_semaphore()

    def greet_y(d, c):
        pl.semaphore_signal(barrier, inc=1, device_id=(ix, lax.rem(iy + d, ny)), device_id_type=MESH)
        return c

    def greet_x(d, c):
        pl.semaphore_signal(barrier, inc=1, device_id=(lax.rem(ix + d, nx), iy), device_id_type=MESH)
        return c

    lax.fori_loop(1, ny, greet_y, 0)
    lax.fori_loop(1, nx, greet_x, 0)

    for t in range(tile_rows):
        rows = start[:, t * tile:(t + 1) * tile]
        ext[0][t] = rows
        first[t] = rows
    for s in range(ghosts):
        outbox[0][s] = first[send_rows[0, s]]
    for j in range(0, steps, 2):
        if j + 1 < steps:
            basis[(j + 1) * width:(j + 2) * width, :] = jnp.zeros((width, basis.shape[1]), BF16)
    pl.semaphore_wait(barrier, nx + ny - 2)

    def halo(j):
        out = []
        sides = (
            (ix < nx - 1, ix > 0, (ix + 1, iy)),
            (ix > 0, ix < nx - 1, (ix - 1, iy)),
            (iy < ny - 1, iy > 0, (ix, iy + 1)),
            (iy > 0, iy < ny - 1, (ix, iy - 1)),
        )
        for n, (sends, receives, peer) in enumerate(sides):
            low = tile_rows + n * ghosts
            copy = pltpu.make_async_remote_copy(
                src_ref=outbox[j], dst_ref=ext[j].at[low:low + ghosts],
                send_sem=halo_send.at[j, n], recv_sem=halo_recv.at[j, n],
                device_id=peer, device_id_type=MESH)
            out.append((sends, receives, copy))
        return out

    def halo_start(j):
        for sends, _, copy in halo(j):
            pl.when(sends)(copy.start)

    def halo_wait(j):
        for _, receives, copy in halo(j):
            pl.when(receives)(copy.wait_recv)

    def halo_drain(j):
        for sends, _, copy in halo(j):
            pl.when(sends)(copy.wait_send)

    def rs_copy(u, d):
        peer = lax.rem(iy + d, ny)
        return pltpu.make_async_remote_copy(
            src_ref=part[u].at[peer], dst_ref=rs[u].at[d],
            send_sem=rs_send.at[u, d], recv_sem=rs_recv.at[u, d],
            device_id=(ix, peer), device_id_type=MESH)

    def xs_copy(u, d):
        return pltpu.make_async_remote_copy(
            src_ref=xs[u].at[0], dst_ref=xs[u].at[d],
            send_sem=xs_send.at[u, d], recv_sem=xs_recv.at[u, d],
            device_id=(lax.rem(ix + d, nx), iy), device_id_type=MESH)

    def ag_copy(u, d):
        return pltpu.make_async_remote_copy(
            src_ref=full[u].at[iy], dst_ref=full[u].at[iy],
            send_sem=ag_send.at[u, d], recv_sem=ag_recv.at[u, d],
            device_id=(ix, lax.rem(iy + d, ny)), device_id_type=MESH)

    def each(count, act):
        def turn(d, c):
            act(d)
            return c
        lax.fori_loop(1, count, turn, 0)

    def phase_1(u):
        each(ny, lambda d: rs_copy(u, d).start())

    def phase_2(u):
        each(ny, lambda d: rs_copy(u, d).wait_recv())
        total_piece = part[u][iy]
        for d in range(1, ny):
            total_piece = total_piece + rs[u][d]
        xs[u][0] = total_piece
        each(nx, lambda d: xs_copy(u, d).start())

    def phase_3(u):
        each(nx, lambda d: xs_copy(u, d).wait_recv())
        total_piece = xs[u][lax.rem(ix, nx)]
        for source in range(1, nx):
            total_piece = total_piece + xs[u][lax.rem(ix - source + nx, nx)]
        full[u][iy] = total_piece
        each(ny, lambda d: ag_copy(u, d).start())

    def phase_4(u):
        each(ny, lambda d: ag_copy(u, d).wait_recv())
        for p in range(ny):
            low = u * width + p * piece
            gram[low:low + piece, :full[u].shape[2]] = full[u][p]

    def drain(u):
        each(ny, lambda d: rs_copy(u, d).wait_send())
        each(nx, lambda d: xs_copy(u, d).wait_send())
        each(ny, lambda d: ag_copy(u, d).wait_send())

    def row_image(j, r):
        acc = nt(ext[j][tile_cols[r, 0]], tiles[r, 0])
        for k in range(1, slots):
            acc = acc + nt(ext[j][tile_cols[r, k]], tiles[r, k])
        return (acc - shifts[j] * ext[j][r].astype(F32)).astype(BF16)

    halo_start(0)
    for t in range(tile_rows):
        tile_copy(t).wait()

    for j in range(steps):
        halo_wait(j)
        if j + 1 < steps:
            for s in range(ghosts):
                outbox[j + 1][s] = row_image(j, send_rows[0, s])
            halo_start(j + 1)

        def row(t, c):
            value = row_image(j, t)
            if j + 1 < steps:
                ext[j + 1][t] = value
            basis[j * width:(j + 1) * width, pl.ds(pl.multiple_of(t * tile, tile), tile)] = value
            return c

        lax.fori_loop(0, tile_rows, row, 0)
        local = nt(basis[j * width:(j + 1) * width, :], basis[0:part[j].shape[2], :]) / total
        for p in range(ny):
            part[j][p] = local[p * piece:(p + 1) * piece]
        phase_1(j)
        if j >= 1:
            phase_2(j - 1)
        if j >= 2:
            phase_3(j - 2)

    last = steps - 1
    phase_2(last)
    if steps > 1:
        phase_3(last - 1)
    phase_3(last)
    for u in range(steps):
        phase_4(u)
    for u in range(steps):
        halo_drain(u)
        drain(u)


def finish_kernel(dims, basis, gram, out, inverse, staged, sem):
    steps, width, chunk = dims
    high = lax.Precision.HIGHEST
    size = steps * width
    inverse[...] = jnp.zeros((size, size), F32)
    rows = lax.broadcasted_iota(jnp.int32, (8, 2 * width), 0)
    eye_r = lax.broadcasted_iota(jnp.int32, (width, width), 0)
    eye_c = lax.broadcasted_iota(jnp.int32, (width, width), 1)
    eye = jnp.where(eye_r == eye_c, 1.0, 0.0).astype(F32)
    for j in range(steps):
        lo, hi = j * width, (j + 1) * width
        block = gram[lo:hi, lo:hi]
        if j:
            previous = inverse[0:lo, 0:lo]
            left = nt(gram[lo:hi, 0:lo], previous, high)
            block = block - nt(left, left, high)
        work = jnp.concatenate([block, eye], axis=1)
        groups = [work[g * 8:(g + 1) * 8] for g in range(width // 8)]
        done = []
        for k in range(width):
            g, r = k // 8, k % 8
            pivot_row = groups[g][r:r + 1]
            pivot = groups[g][r:r + 1, k:k + 1]
            done.append(pivot_row * lax.rsqrt(pivot))
            scaled = pivot_row / pivot
            for h in range(g, width // 8):
                update = groups[h] - groups[h][:, k:k + 1] * scaled
                groups[h] = jnp.where(rows > r, update, groups[h]) if h == g else update
        own = jnp.concatenate(done, axis=0)[:, width:]
        inverse[lo:hi, lo:hi] = own
        if j:
            cross = jnp.dot(left, previous, precision=high, preferred_element_type=F32)
            inverse[lo:hi, 0:lo] = -jnp.dot(own, cross, precision=high, preferred_element_type=F32)
    whole = inverse[...]
    main = whole.astype(BF16)
    rest = (whole - main.astype(F32)).astype(BF16)
    copies = []
    for n in range(basis.shape[1] // chunk):
        cols = slice(n * chunk, (n + 1) * chunk)
        b = basis[:, cols]
        staged[:, cols] = jnp.dot(main, b, preferred_element_type=F32) + jnp.dot(
            rest, b, preferred_element_type=F32)
        copy = pltpu.make_async_copy(staged.at[:, cols], out.at[:, cols], sem.at[n])
        copy.start()
        copies.append(copy)
    for copy in copies:
        copy.wait()


def body(nx, ny, start_block, tiles, tile_cols, send_rows, shifts):
    width, nodes = start_block.shape
    tile_rows, slots, tile, _ = tiles.shape
    ghosts = send_rows.shape[1]
    steps = shifts.shape[0]
    size = steps * width
    piece = width // ny
    dims = (nx, ny, steps, tile_rows, slots, ghosts, tile, width, nodes * nx * ny)
    spans = [-(-(u + 1) * width // 128) * 128 for u in range(steps)]
    dma = pltpu.SemaphoreType.DMA
    vmem = pl.BlockSpec(memory_space=pltpu.VMEM)
    smem = pl.BlockSpec(memory_space=pltpu.SMEM)
    basis, gram = pl.pallas_call(
        functools.partial(krylov_kernel, dims),
        out_shape=(
            jax.ShapeDtypeStruct((size, nodes), BF16),
            jax.ShapeDtypeStruct((size, size), F32),
        ),
        in_specs=[smem, smem, smem, vmem, pl.BlockSpec(memory_space=pl.ANY)],
        out_specs=(vmem, vmem),
        scratch_shapes=[
            pltpu.VMEM(tiles.shape, BF16),
            dma((tile_rows,)),
            dma((steps, 4)), dma((steps, 4)),
            dma((steps, ny)), dma((steps, ny)),
            dma((steps, nx)), dma((steps, nx)),
            dma((steps, ny)), dma((steps, ny)),
        ]
        + [pltpu.VMEM((tile_rows + 4 * ghosts, width, tile), BF16) for _ in range(steps)]
        + [pltpu.VMEM((ghosts, width, tile), BF16) for _ in range(steps)]
        + [pltpu.VMEM((ny, piece, s), F32) for s in spans]
        + [pltpu.VMEM((ny, piece, s), F32) for s in spans]
        + [pltpu.VMEM((nx, piece, s), F32) for s in spans]
        + [pltpu.VMEM((ny, piece, s), F32) for s in spans]
        + [pltpu.VMEM((tile_rows, width, tile), BF16)],
        compiler_params=pltpu.CompilerParams(collective_id=0, has_side_effects=True),
    )(send_rows, tile_cols, shifts, start_block, tiles)
    chunk = 2 * tile
    return pl.pallas_call(
        functools.partial(finish_kernel, (steps, width, chunk)),
        out_shape=jax.ShapeDtypeStruct((size, nodes), F32),
        in_specs=[vmem, vmem],
        out_specs=pl.BlockSpec(memory_space=pl.ANY),
        scratch_shapes=[
            pltpu.VMEM((size, size), F32),
            pltpu.VMEM((size, nodes), F32),
            dma((nodes // chunk,)),
        ],
    )(basis, gram)


def solution(mesh):
    in_specs = (
        P(None, ("gx", "gy")),
        P(("gx", "gy"), None, None, None),
        P(("gx", "gy"), None),
        P(("gx", "gy"), None),
        P(),
    )
    out_specs = P(None, ("gx", "gy"))
    run = functools.partial(body, mesh.shape["gx"], mesh.shape["gy"])
    return jax.shard_map(run, mesh=mesh, in_specs=in_specs, out_specs=out_specs, check_vma=False)
```

```python
import functools

import jax
import jax.numpy as jnp
from jax import lax
from jax.experimental import pallas as pl
from jax.experimental.pallas import tpu as pltpu
from jax.sharding import PartitionSpec as P

MESH = pl.DeviceIdType.MESH
F32 = jnp.float32
BF16 = jnp.bfloat16
NT_DIMS = (((1,), (1,)), ((), ()))


def nt(a, b, precision=None):
    return lax.dot_general(a, b, NT_DIMS, precision=precision, preferred_element_type=F32)


def krylov_kernel(dims, send_rows, tile_cols, shifts, start, tiles_hbm, basis, gram, inverse, *scratch):
    nx, ny, steps, tile_rows, slots, ghosts, tile, width, total = dims
    tiles, tile_sem = scratch[0:2]
    halo_send, halo_recv, rs_send, rs_recv, xs_send, xs_recv, ag_send, ag_recv = scratch[2:10]
    at = 10
    ext = scratch[at:at + steps]
    outbox = scratch[at + steps:at + 2 * steps]
    part = scratch[at + 2 * steps:at + 3 * steps]
    rs = scratch[at + 3 * steps:at + 4 * steps]
    xs = scratch[at + 4 * steps:at + 5 * steps]
    full = scratch[at + 5 * steps:at + 6 * steps]
    first = scratch[at + 6 * steps]
    piece = width // ny
    ix, iy = lax.axis_index("gx"), lax.axis_index("gy")

    def tile_copy(t):
        return pltpu.make_async_copy(tiles_hbm.at[t], tiles.at[t], tile_sem.at[t])

    for t in range(tile_rows):
        tile_copy(t).start()

    for s in range(steps):
        ext[s][tile_rows:] = jnp.zeros(ext[s][tile_rows:].shape, BF16)

    inverse[...] = jnp.zeros(inverse.shape, F32)
    barrier = pltpu.get_barrier_semaphore()

    def greet_y(d, c):
        pl.semaphore_signal(barrier, inc=1, device_id=(ix, lax.rem(iy + d, ny)), device_id_type=MESH)
        return c

    def greet_x(d, c):
        pl.semaphore_signal(barrier, inc=1, device_id=(lax.rem(ix + d, nx), iy), device_id_type=MESH)
        return c

    lax.fori_loop(1, ny, greet_y, 0)
    lax.fori_loop(1, nx, greet_x, 0)

    for t in range(tile_rows):
        rows = start[:, t * tile:(t + 1) * tile]
        ext[0][t] = rows
        first[t] = rows
    for s in range(ghosts):
        outbox[0][s] = first[send_rows[0, s]]
    for j in range(0, steps, 2):
        if j + 1 < steps:
            basis[(j + 1) * width:(j + 2) * width, :] = jnp.zeros((width, basis.shape[1]), BF16)
    pl.semaphore_wait(barrier, nx + ny - 2)

    def halo(j):
        out = []
        sides = (
            (ix < nx - 1, ix > 0, (ix + 1, iy)),
            (ix > 0, ix < nx - 1, (ix - 1, iy)),
            (iy < ny - 1, iy > 0, (ix, iy + 1)),
            (iy > 0, iy < ny - 1, (ix, iy - 1)),
        )
        for n, (sends, receives, peer) in enumerate(sides):
            low = tile_rows + n * ghosts
            copy = pltpu.make_async_remote_copy(
                src_ref=outbox[j], dst_ref=ext[j].at[low:low + ghosts],
                send_sem=halo_send.at[j, n], recv_sem=halo_recv.at[j, n],
                device_id=peer, device_id_type=MESH)
            out.append((sends, receives, copy))
        return out

    def halo_start(j):
        for sends, _, copy in halo(j):
            pl.when(sends)(copy.start)

    def halo_wait(j):
        for _, receives, copy in halo(j):
            pl.when(receives)(copy.wait_recv)

    def halo_drain(j):
        for sends, _, copy in halo(j):
            pl.when(sends)(copy.wait_send)

    def rs_copy(u, d):
        peer = lax.rem(iy + d, ny)
        return pltpu.make_async_remote_copy(
            src_ref=part[u].at[peer], dst_ref=rs[u].at[d],
            send_sem=rs_send.at[u, d], recv_sem=rs_recv.at[u, d],
            device_id=(ix, peer), device_id_type=MESH)

    def xs_copy(u, d):
        return pltpu.make_async_remote_copy(
            src_ref=xs[u].at[0], dst_ref=xs[u].at[d],
            send_sem=xs_send.at[u, d], recv_sem=xs_recv.at[u, d],
            device_id=(lax.rem(ix + d, nx), iy), device_id_type=MESH)

    def ag_copy(u, d):
        return pltpu.make_async_remote_copy(
            src_ref=full[u].at[iy], dst_ref=full[u].at[iy],
            send_sem=ag_send.at[u, d], recv_sem=ag_recv.at[u, d],
            device_id=(ix, lax.rem(iy + d, ny)), device_id_type=MESH)

    def each(count, act):
        def turn(d, c):
            act(d)
            return c
        lax.fori_loop(1, count, turn, 0)

    def phase_1(u):
        each(ny, lambda d: rs_copy(u, d).start())

    def phase_2(u):
        each(ny, lambda d: rs_copy(u, d).wait_recv())
        total_piece = part[u][iy]
        for d in range(1, ny):
            total_piece = total_piece + rs[u][d]
        xs[u][0] = total_piece
        each(nx, lambda d: xs_copy(u, d).start())

    def phase_3(u):
        each(nx, lambda d: xs_copy(u, d).wait_recv())
        total_piece = xs[u][lax.rem(ix, nx)]
        for source in range(1, nx):
            total_piece = total_piece + xs[u][lax.rem(ix - source + nx, nx)]
        full[u][iy] = total_piece
        each(ny, lambda d: ag_copy(u, d).start())

    def phase_4(u):
        each(ny, lambda d: ag_copy(u, d).wait_recv())
        for p in range(ny):
            low = p * piece
            gram[low:low + piece, :full[u].shape[2]] = full[u][p]
        if u + 1 < steps:
            extend_inverse(u, width, gram[:, :(u + 1) * width], inverse)

    def drain(u):
        each(ny, lambda d: rs_copy(u, d).wait_send())
        each(nx, lambda d: xs_copy(u, d).wait_send())
        each(ny, lambda d: ag_copy(u, d).wait_send())

    def row_image(j, r):
        acc = nt(ext[j][tile_cols[r, 0]], tiles[r, 0])
        for k in range(1, slots):
            acc = acc + nt(ext[j][tile_cols[r, k]], tiles[r, k])
        return (acc - shifts[j] * ext[j][r].astype(F32)).astype(BF16)

    halo_start(0)
    for t in range(tile_rows):
        tile_copy(t).wait()

    for j in range(steps):
        halo_wait(j)
        if j + 1 < steps:
            for s in range(ghosts):
                outbox[j + 1][s] = row_image(j, send_rows[0, s])
            halo_start(j + 1)
        if j >= 1:
            phase_2(j - 1)

        def row(t, c):
            value = row_image(j, t)
            if j + 1 < steps:
                ext[j + 1][t] = value
            basis[j * width:(j + 1) * width, pl.ds(pl.multiple_of(t * tile, tile), tile)] = value
            return c

        lax.fori_loop(0, tile_rows, row, 0)
        local = nt(basis[j * width:(j + 1) * width, :], basis[0:part[j].shape[2], :]) / total
        for p in range(ny):
            part[j][p] = local[p * piece:(p + 1) * piece]
        phase_1(j)
        if j >= 1:
            phase_3(j - 1)
        if 2 <= j < steps - 1:
            phase_4(j - 2)

    last = steps - 1
    waiting = list(range(max(0, last - 2), last))
    for act in (phase_2, phase_3):
        if waiting:
            phase_4(waiting.pop(0))
        act(last)
    for u in waiting + [last]:
        phase_4(u)
    for u in range(steps):
        halo_drain(u)
        drain(u)


def factor(block):
    width = block.shape[0]
    count = width // 8
    eye_r = lax.broadcasted_iota(jnp.int32, (width, width), 0)
    eye_c = lax.broadcasted_iota(jnp.int32, (width, width), 1)
    work = jnp.concatenate([block, jnp.where(eye_r == eye_c, 1.0, 0.0).astype(F32)], axis=1)
    rows = lax.broadcasted_iota(jnp.int32, (8, 2 * width), 0)
    groups = [work[g * 8:(g + 1) * 8] for g in range(count)]
    done = []
    for g in range(count):
        cols = [
            [jnp.broadcast_to(groups[h][:, g * 8 + r:g * 8 + r + 1], (8, 2 * width)) for h in range(g, count)]
            for r in range(8)
        ]
        pivots = cols[0][0]
        for r in range(8):
            inverse = 1.0 / cols[r][0][r:r + 1]
            if r:
                pivots = jnp.where(rows == r, cols[r][0], pivots)
            for m in range(r + 1, 8):
                share = cols[m][0][r:r + 1] * inverse
                cols[m] = [c - d * share for c, d in zip(cols[m], cols[r])]
            scaled = groups[g][r:r + 1] * inverse
            for h in range(g, count):
                update = groups[h] - cols[r][h - g] * scaled
                groups[h] = jnp.where(rows > r, update, groups[h]) if h == g else update
        done.append(groups[g] * lax.rsqrt(pivots))
    return jnp.concatenate(done, axis=0)[:, width:]


def extend_inverse(j, width, gram_row, inverse):
    high = lax.Precision.HIGHEST
    lo, hi = j * width, (j + 1) * width
    block = gram_row[:, lo:hi]
    if j:
        previous = inverse[0:lo, 0:lo]
        left = nt(gram_row[:, 0:lo], previous, high)
        block = block - nt(left, left, high)
    own = factor(block)
    inverse[lo:hi, lo:hi] = own
    if j:
        cross = jnp.dot(left, previous, precision=high, preferred_element_type=F32)
        inverse[lo:hi, 0:lo] = -jnp.dot(own, cross, precision=high, preferred_element_type=F32)


def finish_kernel(dims, basis, gram, above, out, inverse, staged, sem):
    steps, width, chunk = dims
    inverse[...] = above[...]
    extend_inverse(steps - 1, width, gram[...], inverse)
    whole = inverse[...]
    main = whole.astype(BF16)
    rest = (whole - main.astype(F32)).astype(BF16)
    copies = []
    for n in range(basis.shape[1] // chunk):
        cols = slice(n * chunk, (n + 1) * chunk)
        b = basis[:, cols]
        staged[:, cols] = jnp.dot(main, b, preferred_element_type=F32) + jnp.dot(
            rest, b, preferred_element_type=F32)
        copy = pltpu.make_async_copy(staged.at[:, cols], out.at[:, cols], sem.at[n])
        copy.start()
        copies.append(copy)
    for copy in copies:
        copy.wait()


def body(nx, ny, start_block, tiles, tile_cols, send_rows, shifts):
    width, nodes = start_block.shape
    tile_rows, slots, tile, _ = tiles.shape
    ghosts = send_rows.shape[1]
    steps = shifts.shape[0]
    size = steps * width
    piece = width // ny
    dims = (nx, ny, steps, tile_rows, slots, ghosts, tile, width, nodes * nx * ny)
    spans = [-(-(u + 1) * width // 128) * 128 for u in range(steps)]
    dma = pltpu.SemaphoreType.DMA
    vmem = pl.BlockSpec(memory_space=pltpu.VMEM)
    smem = pl.BlockSpec(memory_space=pltpu.SMEM)
    basis, gram, above = pl.pallas_call(
        functools.partial(krylov_kernel, dims),
        out_shape=(
            jax.ShapeDtypeStruct((size, nodes), BF16),
            jax.ShapeDtypeStruct((width, spans[-1]), F32),
            jax.ShapeDtypeStruct((size, size), F32),
        ),
        in_specs=[smem, smem, smem, vmem, pl.BlockSpec(memory_space=pl.ANY)],
        out_specs=(vmem, vmem, vmem),
        scratch_shapes=[
            pltpu.VMEM(tiles.shape, BF16),
            dma((tile_rows,)),
            dma((steps, 4)), dma((steps, 4)),
            dma((steps, ny)), dma((steps, ny)),
            dma((steps, nx)), dma((steps, nx)),
            dma((steps, ny)), dma((steps, ny)),
        ]
        + [pltpu.VMEM((tile_rows + 4 * ghosts, width, tile), BF16) for _ in range(steps)]
        + [pltpu.VMEM((ghosts, width, tile), BF16) for _ in range(steps)]
        + [pltpu.VMEM((ny, piece, s), F32) for s in spans]
        + [pltpu.VMEM((ny, piece, s), F32) for s in spans]
        + [pltpu.VMEM((nx, piece, s), F32) for s in spans]
        + [pltpu.VMEM((ny, piece, s), F32) for s in spans]
        + [pltpu.VMEM((tile_rows, width, tile), BF16)],
        compiler_params=pltpu.CompilerParams(collective_id=0, has_side_effects=True),
    )(send_rows, tile_cols, shifts, start_block, tiles)
    chunk = 2 * tile
    return pl.pallas_call(
        functools.partial(finish_kernel, (steps, width, chunk)),
        out_shape=jax.ShapeDtypeStruct((size, nodes), F32),
        in_specs=[vmem, vmem, vmem],
        out_specs=pl.BlockSpec(memory_space=pl.ANY),
        scratch_shapes=[
            pltpu.VMEM((size, size), F32),
            pltpu.VMEM((size, nodes), F32),
            dma((nodes // chunk,)),
        ],
    )(basis, gram, above)


def solution(mesh):
    in_specs = (
        P(None, ("gx", "gy")),
        P(("gx", "gy"), None, None, None),
        P(("gx", "gy"), None),
        P(("gx", "gy"), None),
        P(),
    )
    out_specs = P(None, ("gx", "gy"))
    run = functools.partial(body, mesh.shape["gx"], mesh.shape["gy"])
    return jax.shard_map(run, mesh=mesh, in_specs=in_specs, out_specs=out_specs, check_vma=False)
```

```python
import functools

import jax
import jax.numpy as jnp
from jax import lax
from jax.experimental import pallas as pl
from jax.experimental.pallas import tpu as pltpu
from jax.sharding import PartitionSpec as P

MESH = pl.DeviceIdType.MESH
F32 = jnp.float32
BF16 = jnp.bfloat16
NT_DIMS = (((1,), (1,)), ((), ()))


def nt(a, b, precision=None):
    return lax.dot_general(a, b, NT_DIMS, precision=precision, preferred_element_type=F32)


def krylov_kernel(dims, send_rows, tile_cols, shifts, start, tiles_hbm, basis, gram, inverse, *scratch):
    nx, ny, steps, tile_rows, slots, ghosts, tile, width, total = dims
    tiles, tile_sem = scratch[0:2]
    halo_send, halo_recv, rs_send, rs_recv, xs_send, xs_recv, ag_send, ag_recv = scratch[2:10]
    at = 10
    ext = scratch[at:at + steps]
    outbox = scratch[at + steps:at + 2 * steps]
    part = scratch[at + 2 * steps:at + 3 * steps]
    rs = scratch[at + 3 * steps:at + 4 * steps]
    xs = scratch[at + 4 * steps:at + 5 * steps]
    full = scratch[at + 5 * steps:at + 6 * steps]
    first = scratch[at + 6 * steps]
    piece = width // ny
    ix, iy = lax.axis_index("gx"), lax.axis_index("gy")

    def tile_copy(t):
        return pltpu.make_async_copy(tiles_hbm.at[t], tiles.at[t], tile_sem.at[t])

    for t in range(tile_rows):
        tile_copy(t).start()

    for s in range(steps):
        ext[s][tile_rows:] = jnp.zeros(ext[s][tile_rows:].shape, BF16)

    inverse[...] = jnp.zeros(inverse.shape, F32)
    barrier = pltpu.get_barrier_semaphore()

    def greet_y(d, c):
        pl.semaphore_signal(barrier, inc=1, device_id=(ix, lax.rem(iy + d, ny)), device_id_type=MESH)
        return c

    def greet_x(d, c):
        pl.semaphore_signal(barrier, inc=1, device_id=(lax.rem(ix + d, nx), iy), device_id_type=MESH)
        return c

    lax.fori_loop(1, ny, greet_y, 0)
    lax.fori_loop(1, nx, greet_x, 0)

    for t in range(tile_rows):
        rows = start[:, t * tile:(t + 1) * tile]
        ext[0][t] = rows
        first[t] = rows
    for s in range(ghosts):
        outbox[0][s] = first[send_rows[0, s]]
    for j in range(0, steps, 2):
        if j + 1 < steps:
            basis[(j + 1) * width:(j + 2) * width, :] = jnp.zeros((width, basis.shape[1]), BF16)
    pl.semaphore_wait(barrier, nx + ny - 2)

    def halo(j):
        out = []
        sides = (
            (ix < nx - 1, ix > 0, (ix + 1, iy)),
            (ix > 0, ix < nx - 1, (ix - 1, iy)),
            (iy < ny - 1, iy > 0, (ix, iy + 1)),
            (iy > 0, iy < ny - 1, (ix, iy - 1)),
        )
        for n, (sends, receives, peer) in enumerate(sides):
            low = tile_rows + n * ghosts
            copy = pltpu.make_async_remote_copy(
                src_ref=outbox[j], dst_ref=ext[j].at[low:low + ghosts],
                send_sem=halo_send.at[j, n], recv_sem=halo_recv.at[j, n],
                device_id=peer, device_id_type=MESH)
            out.append((sends, receives, copy))
        return out

    def halo_start(j):
        for sends, _, copy in halo(j):
            pl.when(sends)(copy.start)

    def halo_wait(j):
        for _, receives, copy in halo(j):
            pl.when(receives)(copy.wait_recv)

    def halo_drain(j):
        for sends, _, copy in halo(j):
            pl.when(sends)(copy.wait_send)

    def rs_copy(u, d):
        peer = lax.rem(iy + d, ny)
        return pltpu.make_async_remote_copy(
            src_ref=part[u].at[peer], dst_ref=rs[u].at[d],
            send_sem=rs_send.at[u, d], recv_sem=rs_recv.at[u, d],
            device_id=(ix, peer), device_id_type=MESH)

    def xs_copy(u, d):
        return pltpu.make_async_remote_copy(
            src_ref=xs[u].at[0], dst_ref=xs[u].at[d],
            send_sem=xs_send.at[u, d], recv_sem=xs_recv.at[u, d],
            device_id=(lax.rem(ix + d, nx), iy), device_id_type=MESH)

    def ag_copy(u, d):
        return pltpu.make_async_remote_copy(
            src_ref=full[u].at[iy], dst_ref=full[u].at[iy],
            send_sem=ag_send.at[u, d], recv_sem=ag_recv.at[u, d],
            device_id=(ix, lax.rem(iy + d, ny)), device_id_type=MESH)

    def each(count, act):
        def turn(d, c):
            act(d)
            return c
        lax.fori_loop(1, count, turn, 0)

    def phase_1(u):
        each(ny, lambda d: rs_copy(u, d).start())

    def phase_2(u):
        each(ny, lambda d: rs_copy(u, d).wait_recv())
        total_piece = part[u][iy]
        for d in range(1, ny):
            total_piece = total_piece + rs[u][d]
        xs[u][0] = total_piece
        each(nx, lambda d: xs_copy(u, d).start())

    def phase_3(u):
        each(nx, lambda d: xs_copy(u, d).wait_recv())
        total_piece = xs[u][lax.rem(ix, nx)]
        for source in range(1, nx):
            total_piece = total_piece + xs[u][lax.rem(ix - source + nx, nx)]
        full[u][iy] = total_piece
        each(ny, lambda d: ag_copy(u, d).start())

    def phase_4(u):
        each(ny, lambda d: ag_copy(u, d).wait_recv())
        for p in range(ny):
            low = p * piece
            gram[low:low + piece, :full[u].shape[2]] = full[u][p]
        if u + 1 < steps:
            extend_inverse(u, width, gram[:, :(u + 1) * width], inverse)

    def drain(u):
        each(ny, lambda d: rs_copy(u, d).wait_send())
        each(nx, lambda d: xs_copy(u, d).wait_send())
        each(ny, lambda d: ag_copy(u, d).wait_send())

    def row_image(j, r):
        acc = jnp.dot(ext[j][tile_cols[r, 0]], tiles[r, 0], preferred_element_type=F32)
        for k in range(1, slots):
            acc = acc + jnp.dot(ext[j][tile_cols[r, k]], tiles[r, k], preferred_element_type=F32)
        return (acc - shifts[j] * ext[j][r].astype(F32)).astype(BF16)

    halo_start(0)

    def turned(t, c):
        tile_copy(t).wait()
        for k in range(slots):
            tiles[t, k] = tiles[t, k].T
        return c

    lax.fori_loop(0, tile_rows, turned, 0)

    for j in range(steps):
        halo_wait(j)
        if j + 1 < steps:
            for s in range(ghosts):
                outbox[j + 1][s] = row_image(j, send_rows[0, s])
            halo_start(j + 1)
        if j >= 1:
            phase_2(j - 1)

        def row(t, c):
            value = row_image(j, t)
            if j + 1 < steps:
                ext[j + 1][t] = value
            basis[j * width:(j + 1) * width, pl.ds(pl.multiple_of(t * tile, tile), tile)] = value
            return c

        lax.fori_loop(0, tile_rows, row, 0, unroll=4)
        local = nt(basis[j * width:(j + 1) * width, :], basis[0:part[j].shape[2], :]) / total
        for p in range(ny):
            part[j][p] = local[p * piece:(p + 1) * piece]
        phase_1(j)
        if j >= 1:
            phase_3(j - 1)
        if 2 <= j < steps - 1:
            phase_4(j - 2)

    last = steps - 1
    waiting = list(range(max(0, last - 2), last))
    for act in (phase_2, phase_3):
        if waiting:
            phase_4(waiting.pop(0))
        act(last)
    for u in waiting + [last]:
        phase_4(u)
    for u in range(steps):
        halo_drain(u)
        drain(u)


def factor(block):
    width = block.shape[0]
    count = width // 8
    eye_r = lax.broadcasted_iota(jnp.int32, (width, width), 0)
    eye_c = lax.broadcasted_iota(jnp.int32, (width, width), 1)
    work = jnp.concatenate([block, jnp.where(eye_r == eye_c, 1.0, 0.0).astype(F32)], axis=1)
    rows = lax.broadcasted_iota(jnp.int32, (8, 2 * width), 0)
    groups = [work[g * 8:(g + 1) * 8] for g in range(count)]
    done = []
    for g in range(count):
        cols = [
            [jnp.broadcast_to(groups[h][:, g * 8 + r:g * 8 + r + 1], (8, 2 * width)) for h in range(g, count)]
            for r in range(8)
        ]
        pivots = cols[0][0]
        for r in range(8):
            inverse = 1.0 / cols[r][0][r:r + 1]
            if r:
                pivots = jnp.where(rows == r, cols[r][0], pivots)
            for m in range(r + 1, 8):
                share = cols[m][0][r:r + 1] * inverse
                cols[m] = [c - d * share for c, d in zip(cols[m], cols[r])]
            scaled = groups[g][r:r + 1] * inverse
            for h in range(g, count):
                update = groups[h] - cols[r][h - g] * scaled
                groups[h] = jnp.where(rows > r, update, groups[h]) if h == g else update
        done.append(groups[g] * lax.rsqrt(pivots))
    return jnp.concatenate(done, axis=0)[:, width:]


def extend_inverse(j, width, gram_row, inverse):
    high = lax.Precision.HIGHEST
    lo, hi = j * width, (j + 1) * width
    block = gram_row[:, lo:hi]
    if j:
        previous = inverse[0:lo, 0:lo]
        left = nt(gram_row[:, 0:lo], previous, high)
        block = block - nt(left, left, high)
    own = factor(block)
    inverse[lo:hi, lo:hi] = own
    if j:
        cross = jnp.dot(left, previous, precision=high, preferred_element_type=F32)
        inverse[lo:hi, 0:lo] = -jnp.dot(own, cross, precision=high, preferred_element_type=F32)


def finish_kernel(dims, basis, gram, above, out, inverse, staged, sem):
    steps, width, chunk = dims
    inverse[...] = above[...]
    extend_inverse(steps - 1, width, gram[...], inverse)
    whole = inverse[...]
    main = whole.astype(BF16)
    rest = (whole - main.astype(F32)).astype(BF16)
    copies = []
    for n in range(basis.shape[1] // chunk):
        cols = slice(n * chunk, (n + 1) * chunk)
        b = basis[:, cols]
        staged[:, cols] = jnp.dot(main, b, preferred_element_type=F32) + jnp.dot(
            rest, b, preferred_element_type=F32)
        copy = pltpu.make_async_copy(staged.at[:, cols], out.at[:, cols], sem.at[n])
        copy.start()
        copies.append(copy)
    for copy in copies:
        copy.wait()


def body(nx, ny, start_block, tiles, tile_cols, send_rows, shifts):
    width, nodes = start_block.shape
    tile_rows, slots, tile, _ = tiles.shape
    ghosts = send_rows.shape[1]
    steps = shifts.shape[0]
    size = steps * width
    piece = width // ny
    dims = (nx, ny, steps, tile_rows, slots, ghosts, tile, width, nodes * nx * ny)
    spans = [-(-(u + 1) * width // 128) * 128 for u in range(steps)]
    dma = pltpu.SemaphoreType.DMA
    vmem = pl.BlockSpec(memory_space=pltpu.VMEM)
    smem = pl.BlockSpec(memory_space=pltpu.SMEM)
    basis, gram, above = pl.pallas_call(
        functools.partial(krylov_kernel, dims),
        out_shape=(
            jax.ShapeDtypeStruct((size, nodes), BF16),
            jax.ShapeDtypeStruct((width, spans[-1]), F32),
            jax.ShapeDtypeStruct((size, size), F32),
        ),
        in_specs=[smem, smem, smem, vmem, pl.BlockSpec(memory_space=pl.ANY)],
        out_specs=(vmem, vmem, vmem),
        scratch_shapes=[
            pltpu.VMEM(tiles.shape, BF16),
            dma((tile_rows,)),
            dma((steps, 4)), dma((steps, 4)),
            dma((steps, ny)), dma((steps, ny)),
            dma((steps, nx)), dma((steps, nx)),
            dma((steps, ny)), dma((steps, ny)),
        ]
        + [pltpu.VMEM((tile_rows + 4 * ghosts, width, tile), BF16) for _ in range(steps)]
        + [pltpu.VMEM((ghosts, width, tile), BF16) for _ in range(steps)]
        + [pltpu.VMEM((ny, piece, s), F32) for s in spans]
        + [pltpu.VMEM((ny, piece, s), F32) for s in spans]
        + [pltpu.VMEM((nx, piece, s), F32) for s in spans]
        + [pltpu.VMEM((ny, piece, s), F32) for s in spans]
        + [pltpu.VMEM((tile_rows, width, tile), BF16)],
        compiler_params=pltpu.CompilerParams(collective_id=0, has_side_effects=True),
    )(send_rows, tile_cols, shifts, start_block, tiles)
    chunk = 2 * tile
    return pl.pallas_call(
        functools.partial(finish_kernel, (steps, width, chunk)),
        out_shape=jax.ShapeDtypeStruct((size, nodes), F32),
        in_specs=[vmem, vmem, vmem],
        out_specs=pl.BlockSpec(memory_space=pl.ANY),
        scratch_shapes=[
            pltpu.VMEM((size, size), F32),
            pltpu.VMEM((size, nodes), F32),
            dma((nodes // chunk,)),
        ],
    )(basis, gram, above)


def solution(mesh):
    in_specs = (
        P(None, ("gx", "gy")),
        P(("gx", "gy"), None, None, None),
        P(("gx", "gy"), None),
        P(("gx", "gy"), None),
        P(),
    )
    out_specs = P(None, ("gx", "gy"))
    run = functools.partial(body, mesh.shape["gx"], mesh.shape["gy"])
    return jax.shard_map(run, mesh=mesh, in_specs=in_specs, out_specs=out_specs, check_vma=False)
```
